256 devices in a mesh: stream: 16 (over y, z_hi, core), span: 16 (over z_lo, x).
Axes of the slice: x: 4, y: 4, z: 8 (z_hi: 2, z_lo: 4; z = z_hi * 4 + z_lo), core: 2. Of those that a mesh axis runs over, the one named last changes fastest.
Arguments:
- velocity_modes: bfloat16 [32, 128, 10, 3, 128], P('stream', 'span'), may hold values from -6 to 6
- cell_weight: float32 [32, 128, 10], P('stream', 'span'), may hold values from 0.001 to 0.01
Outputs:
- convection: float32 [128, 128, 128], replicated
The draws below stay inside these ranges and needn't reach their ends.
All inputs are finite; a program needn't handle non-finite values.
Results may differ from the reference program's by a relative error of at most 0.0085.
Values may be sent and summed in bfloat16 or wider, within the bound.
A program may use at most 64 MiB of HBM per device.

```python
import math
import jax
import jax.numpy as jnp
from jax import lax

M = 128
NZ = 10
NX = 32
NY = 128


def levels(own_key, extent, pieces, least, largest):
    loudness = 1.0
    for position, parts in pieces:
        heights = jax.random.uniform(jax.random.fold_in(jax.random.fold_in(own_key, 6), position), (parts,), jnp.float32, least / len(pieces), largest / len(pieces))
        loudness = loudness * jnp.repeat(jnp.exp(heights), extent[position] // parts).reshape((-1,) + (1,) * (len(extent) - 1 - position))
    return loudness


def scatter_about(stream_key, dims, deviation, most, split=(), dtype=jnp.bfloat16):
    result = deviation * jax.random.normal(stream_key, dims, jnp.float32)
    if split:
        result = result * levels(stream_key, dims, split, -0.22, 0.18)
    return jnp.clip(result, -most, most).astype(dtype)


def setup_inputs(seed: int = 0) -> dict:
    key_list = jax.random.split(jax.random.key(seed), 3)
    velocity_modes = scatter_about(key_list[0], (NX, NY, NZ, 3, M), 1.0, 6.0, ((0, 16), (1, 16)))
    cell_weight = jnp.clip(jnp.exp(math.log(0.01) - 2.30258502 * jax.random.uniform(key_list[1], (NX, NY, NZ), jnp.float32) ** levels(key_list[1], (NX, NY, NZ), ((0, 16), (1, 16)), -0.2, 0.2)), 0.001, 0.01)
    return {"velocity_modes": velocity_modes, "cell_weight": cell_weight}


def gradient(padded):
    core_x = padded[:, 2:-2]
    deriv_x = (8.0 * (core_x[3:-1] - core_x[1:-3]) - (core_x[4:] - core_x[:-4])) / 12.0
    core_y = padded[2:-2]
    deriv_y = (8.0 * (core_y[:, 3:-1] - core_y[:, 1:-3]) - (core_y[:, 4:] - core_y[:, :-4])) / 12.0
    center = padded[2:-2, 2:-2]
    vertical = jnp.pad(center, ((0, 0), (0, 0), (1, 1), (0, 0), (0, 0)))
    deriv_z = 0.5 * (vertical[:, :, 2:] - vertical[:, :, :-2])
    return jnp.stack([deriv_x, deriv_y, deriv_z])


def reference(velocity_modes, cell_weight):
    phi_full = velocity_modes.astype(jnp.float32)
    padded = jnp.pad(phi_full, ((2, 2), (2, 2), (0, 0), (0, 0), (0, 0)))
    grads = gradient(padded)
    width = phi_full.shape[-1]
    plane = NY * NZ

    def add_slice(slice_index, running):
        phi_x = lax.dynamic_index_in_dim(phi_full, slice_index, 0, False).reshape(plane, 3, width)
        grad_x = lax.dynamic_index_in_dim(grads, slice_index, 1, False).reshape(3, plane, 3, width)
        weight_x = lax.dynamic_index_in_dim(cell_weight, slice_index, 0, False).reshape(plane)
        quad = jnp.einsum("cbi,acbk->acik", phi_x, grad_x, precision=lax.Precision.HIGHEST)
        quad = quad * weight_x[None, :, None, None]
        quad = lax.optimization_barrier(quad.astype(jnp.bfloat16)).astype(jnp.float32)
        return running + jnp.einsum("caj,acik->ijk", phi_x, quad, precision=lax.Precision.HIGHEST)

    zeros = jnp.zeros((width, width, width), jnp.float32)
    return lax.fori_loop(0, NX, add_slice, zeros)
```

```python
import jax
import jax.numpy as jnp
from jax import lax
from jax.experimental import pallas as pl
from jax.experimental.pallas import tpu as pltpu
from jax.sharding import PartitionSpec as P

MESH = pl.DeviceIdType.MESH
F32, BF16 = jnp.float32, jnp.bfloat16
M = 128
NX, NY, NZ = 2, 8, 10
CELLS = NX * NY * NZ
HALF = M // 2
ROWS = HALF * M
CX, CY, CZH, CZL = 4, 4, 2, 4
CZ = CZH * CZL
VMEM = pl.BlockSpec(memory_space=pltpu.VMEM)


def coords():
    s, p = lax.axis_index("stream"), lax.axis_index("span")
    core = lax.rem(s, 2)
    zh = lax.rem(s // 2, CZH)
    y = s // (2 * CZH)
    zl = p // CX
    x = lax.rem(p, CX)
    return x, y, zh * CZL + zl, core


def device(x, y, z, core):
    return ((y * CZH + z // CZL) * 2 + core, lax.rem(z, CZL) * CX + x)


def halo_kernel(phi_ref, w_ref, x_ref, halo, ext, send_sem, recv_sem):
    s, p = lax.axis_index("stream"), lax.axis_index("span")
    ns, np_ = lax.axis_size("stream"), lax.axis_size("span")
    core = lax.rem(s, 2)
    partner = (s + 1 - 2 * core, p)
    before, after = (lax.rem(s + ns - 1, ns), p), (lax.rem(s + 1, ns), p)
    left, right = (s, lax.rem(p + np_ - 1, np_)), (s, lax.rem(p + 1, np_))

    barrier = pltpu.get_barrier_semaphore()
    for peer in (before, after, left, right):
        pl.semaphore_signal(barrier, inc=1, device_id=peer, device_id_type=MESH)
    pl.semaphore_wait(barrier, 4)

    copies = []
    for slot, peer in ((1, before), (0, after), (3, left), (2, right)):
        copy = pltpu.make_async_remote_copy(
            src_ref=phi_ref,
            dst_ref=halo.at[slot],
            send_sem=send_sem.at[slot],
            recv_sem=recv_sem.at[slot],
            device_id=peer,
            device_id_type=MESH,
        )
        copy.start()
        copies.append(copy)
    from_after, from_before, from_right, from_left = copies[0], copies[1], copies[2], copies[3]

    def weight(x, z):
        return jnp.broadcast_to(w_ref[x, :, z : z + 1], (NY, M))

    def rows(x, z):
        return pl.ds((x * NZ + z) * NY, NY)

    zero = jnp.zeros((NY, M), F32)

    def own(x, z, b):
        return phi_ref[x, z, b].astype(F32)

    for x in range(NX):
        for z in range(NZ):
            for b in range(3):
                x_ref[b, core, rows(x, z), :] = phi_ref[x, z, b]
                up = own(x, z + 1, b) if z + 1 < NZ else zero
                down = own(x, z - 1, b) if z > 0 else zero
                grad = 0.5 * (up - down) * weight(x, z)
                x_ref[9 + b, core, rows(x, z), :] = grad.astype(BF16)

    from_left.wait()
    from_right.wait()
    has_left = (p > 0).astype(F32)
    has_right = (p < np_ - 1).astype(F32)
    for x in range(NX):
        for z in range(NZ):
            for b in range(3):
                ext[0:NY] = halo[2, x, z, b].astype(F32) * has_left
                ext[NY : 2 * NY] = own(x, z, b)
                ext[2 * NY : 3 * NY] = halo[3, x, z, b].astype(F32) * has_right
                near = ext[NY + 1 : 2 * NY + 1] - ext[NY - 1 : 2 * NY - 1]
                far = ext[NY + 2 : 2 * NY + 2] - ext[NY - 2 : 2 * NY - 2]
                grad = (8.0 * near - far) * (weight(x, z) * (1.0 / 12.0))
                x_ref[6 + b, core, rows(x, z), :] = grad.astype(BF16)

    def to_partner(k, first, count):
        copy = pltpu.make_async_remote_copy(
            src_ref=x_ref.at[pl.ds(first, count), core],
            dst_ref=x_ref.at[pl.ds(first, count), core],
            send_sem=send_sem.at[k],
            recv_sem=recv_sem.at[k],
            device_id=partner,
            device_id_type=MESH,
        )
        copy.start()
        return copy

    pair = [to_partner(4, 0, 3), to_partner(5, 6, 6)]

    from_before.wait()
    from_after.wait()
    has_before = (s > 0).astype(F32)
    has_after = (s < ns - 1).astype(F32)
    for z in range(NZ):
        for b in range(3):
            a0 = halo[0, 0, z, b].astype(F32) * has_before
            a1 = halo[0, 1, z, b].astype(F32) * has_before
            c0, c1 = own(0, z, b), own(1, z, b)
            d0 = halo[1, 0, z, b].astype(F32) * has_after
            d1 = halo[1, 1, z, b].astype(F32) * has_after
            g0 = (8.0 * (c1 - a1) - (d0 - a0)) * (weight(0, z) * (1.0 / 12.0))
            g1 = (8.0 * (d0 - c0) - (d1 - a1)) * (weight(1, z) * (1.0 / 12.0))
            x_ref[3 + b, core, rows(0, z), :] = g0.astype(BF16)
            x_ref[3 + b, core, rows(1, z), :] = g1.astype(BF16)
    pair.append(to_partner(6, 3, 3))
    for copy in pair:
        copy.wait()


def halo_call(phi, weight):
    return pl.pallas_call(
        halo_kernel,
        out_shape=jax.ShapeDtypeStruct((12, 2, CELLS, M), BF16),
        in_specs=[VMEM, VMEM],
        out_specs=VMEM,
        scratch_shapes=[
            pltpu.VMEM((4, NX, NZ, 3, NY, M), BF16),
            pltpu.VMEM((3 * NY, M), F32),
            pltpu.SemaphoreType.DMA((7,)),
            pltpu.SemaphoreType.DMA((7,)),
        ],
        compiler_params=pltpu.CompilerParams(collective_id=0, has_side_effects=True),
        name="halo",
    )(phi, weight)


BLOCK = 4
TILES = 8


def product_kernel(x_ref, out_ref, phi_i, grad, test, quad_a, quad_b):
    core = lax.rem(lax.axis_index("stream"), 2)
    flat = x_ref

    def piece(q, first, count):
        dev, row = first // CELLS, first % CELLS
        if row + count <= CELLS:
            return flat[q, dev, row : row + count, :]
        head = CELLS - row
        return jnp.concatenate(
            [flat[q, dev, row:CELLS, :], flat[q, dev + 1, 0 : count - head, :]], axis=0
        )

    def tile(base, stride, t):
        if t < 6:
            return piece(base + stride * (t // 2), (t % 2) * M, M)
        if t == 6:
            return jnp.concatenate(
                [piece(base, 2 * M, 64), piece(base + stride, 2 * M, 64)], axis=0
            )
        return jnp.concatenate(
            [piece(base + 2 * stride, 2 * M, 64), jnp.zeros((64, M), BF16)], axis=0
        )

    for t in range(TILES):
        test[t * M : (t + 1) * M, :] = tile(0, 1, t)
        for b in range(3):
            grad[b, t] = tile(3 + b, 3, t).astype(F32).T
    for b in range(3):
        for half in range(3):
            if half < 2:
                cells = piece(b, half * M, M)
            else:
                tail = piece(b, 2 * M, 64)
                cells = jnp.concatenate([tail, tail], axis=0)
            phi_i[b, half] = cells.astype(F32).T

    def quads(block, quad):
        for t in range(TILES):
            half = t % 2 if t < 6 else 2
            for n in range(BLOCK):
                i = core * HALF + block * BLOCK + n
                q = phi_i[0, half, pl.ds(i, 1), :] * grad[0, t]
                q = q + phi_i[1, half, pl.ds(i, 1), :] * grad[1, t]
                q = q + phi_i[2, half, pl.ds(i, 1), :] * grad[2, t]
                quad[n * M : (n + 1) * M, t * M : (t + 1) * M] = q.astype(BF16)

    def contract(block, quad):
        res = jnp.dot(quad[...], test[...], preferred_element_type=F32)
        for n in range(BLOCK):
            first = pl.multiple_of((block * BLOCK + n) * M, M)
            out_ref[pl.ds(first, M), :] = res[n * M : (n + 1) * M].T.astype(BF16)

    blocks = HALF // BLOCK
    quads(0, quad_a)

    @pl.loop(0, blocks // 2 - 1)
    def _(turn):
        quads(2 * turn + 1, quad_b)
        contract(2 * turn, quad_a)
        quads(2 * turn + 2, quad_a)
        contract(2 * turn + 1, quad_b)

    quads(blocks - 1, quad_b)
    contract(blocks - 2, quad_a)
    contract(blocks - 1, quad_b)


def product_call(gathered):
    return pl.pallas_call(
        product_kernel,
        out_shape=jax.ShapeDtypeStruct((ROWS, M), BF16),
        in_specs=[VMEM],
        out_specs=VMEM,
        scratch_shapes=[
            pltpu.VMEM((3, 3, M, M), F32),
            pltpu.VMEM((3, TILES, M, M), F32),
            pltpu.VMEM((TILES * M, M), BF16),
            pltpu.VMEM((BLOCK * M, TILES * M), BF16),
            pltpu.VMEM((BLOCK * M, TILES * M), BF16),
        ],
        name="product",
    )(gathered)


CHUNKS = 4
CH = ROWS // CHUNKS
N1, N2, N3 = CH // 4, CH // 16, CH // 128


def sum_kernel(part_ref, full_ref, got1, got2, got3, sum1, sum2, send_sem, recv_sem):
    x, y, z, core = coords()
    u = x * (1 - core) + y * core
    v = y * (1 - core) + x * core

    def along_u(d):
        return device(lax.rem(x + d * (1 - core), CX), lax.rem(y + d * core, CY), z, core)

    def along_v(d):
        return device(lax.rem(x + d * core, CX), lax.rem(y + d * (1 - core), CY), z, core)

    def along_z(d):
        return device(x, y, lax.rem(z + d, CZ), core)

    partner = device(x, y, z, 1 - core)
    barrier = pltpu.get_barrier_semaphore()
    peers = [along_u(d) for d in (1, 2, 3)] + [along_v(d) for d in (1, 2, 3)]
    peers += [along_z(d) for d in range(1, CZ)] + [partner]
    for peer in peers:
        pl.semaphore_signal(barrier, inc=1, device_id=peer, device_id_type=MESH)
    pl.semaphore_wait(barrier, len(peers))

    def send(src, dst, c, k, peer):
        copy = pltpu.make_async_remote_copy(
            src_ref=src,
            dst_ref=dst,
            send_sem=send_sem.at[c, k],
            recv_sem=recv_sem.at[c, k],
            device_id=peer,
            device_id_type=MESH,
        )
        copy.start()
        return copy

    flying = {}

    def block(first, count):
        return pl.ds(pl.multiple_of(first, count), count)

    def stage0(c):
        flying[c, 0] = [
            send(
                part_ref.at[block(c * CH + lax.rem(u + d, 4) * N1, N1)],
                got1.at[c, d - 1],
                c,
                d - 1,
                along_u(d),
            )
            for d in (2, 1, 3)
        ]

    def stage1(c):
        for copy in flying[c, 0]:
            copy.wait()
        total = part_ref[block(c * CH + u * N1, N1), :].astype(F32)
        for d in range(3):
            total = total + got1[c, d].astype(F32)
        sum1[c] = total.astype(BF16)
        flying[c, 1] = [
            send(
                sum1.at[c, block(lax.rem(v + d, 4) * N2, N2)], got2.at[c, d - 1], c, 2 + d, along_v(d)
            )
            for d in (2, 1, 3)
        ]

    def stage2(c):
        for copy in flying[c, 1]:
            copy.wait()
        total = sum1[c, block(v * N2, N2), :].astype(F32)
        for d in range(3):
            total = total + got2[c, d].astype(F32)
        sum2[c] = total.astype(BF16)
        flying[c, 2] = [
            send(
                sum2.at[c, block(lax.rem(z + d, CZ) * N3, N3)], got3.at[c, d - 1], c, 5 + d, along_z(d)
            )
            for d in (4, 3, 5, 2, 6, 1, 7)
        ]

    def mine(c, uu, vv, zz):
        return c * CH + uu * N1 + vv * N2 + zz * N3

    def stage3(c):
        for copy in flying[c, 2]:
            copy.wait()
        total = sum2[c, block(z * N3, N3), :].astype(F32)
        for d in range(CZ - 1):
            total = total + got3[c, d].astype(F32)
        shard = full_ref.at[core, block(mine(c, u, v, z), N3)]
        full_ref[core, block(mine(c, u, v, z), N3), :] = total.astype(BF16)
        flying[c, 3] = [send(shard, shard, c, 12 + d, along_z(d)) for d in (4, 3, 5, 2, 6, 1, 7)]

    def stage4(c):
        for copy in flying[c, 3]:
            copy.wait()
        piece = full_ref.at[core, block(mine(c, u, v, 0), N2)]
        flying[c, 4] = [send(piece, piece, c, 19 + d, along_v(d)) for d in (2, 1, 3)]

    def stage5(c):
        for copy in flying[c, 4]:
            copy.wait()
        piece = full_ref.at[core, block(mine(c, u, 0, 0), N1)]
        flying[c, 5] = [send(piece, piece, c, 22 + d, along_u(d)) for d in (2, 1, 3)]

    def stage6(c):
        for copy in flying[c, 5]:
            copy.wait()
        piece = full_ref.at[core, pl.ds(c * CH, CH)]
        flying[c, 6] = [send(piece, piece, c, 26, partner)]

    def stage7(c):
        for copy in flying[c, 6]:
            copy.wait()

    stages = [stage0, stage1, stage2, stage3, stage4, stage5, stage6, stage7]
    for turn in range(CHUNKS + len(stages) - 1):
        for k in reversed(range(len(stages))):
            if 0 <= turn - k < CHUNKS:
                stages[k](turn - k)


def sum_call(part):
    return pl.pallas_call(
        sum_kernel,
        out_shape=jax.ShapeDtypeStruct((2, ROWS, M), BF16),
        in_specs=[VMEM],
        out_specs=VMEM,
        scratch_shapes=[
            pltpu.VMEM((CHUNKS, 3, N1, M), BF16),
            pltpu.VMEM((CHUNKS, 3, N2, M), BF16),
            pltpu.VMEM((CHUNKS, CZ - 1, N3, M), BF16),
            pltpu.VMEM((CHUNKS, N1, M), BF16),
            pltpu.VMEM((CHUNKS, N2, M), BF16),
            pltpu.SemaphoreType.DMA((CHUNKS, 27)),
            pltpu.SemaphoreType.DMA((CHUNKS, 27)),
        ],
        compiler_params=pltpu.CompilerParams(collective_id=1, has_side_effects=True),
        name="sum",
    )(part)


def shards(velocity_modes, cell_weight):
    phi = jnp.transpose(velocity_modes, (0, 2, 3, 1, 4))
    gathered = halo_call(phi, cell_weight)
    part = product_call(gathered)
    full = sum_call(part)
    return full.reshape(M, M, M).astype(F32)


def solution(mesh):
    placed = (P("stream", "span", None, None, None), P("stream", "span", None))
    return jax.shard_map(shards, mesh=mesh, in_specs=placed, out_specs=P(), check_vma=False)
```

```python
import jax
import jax.numpy as jnp
from jax import lax
from jax.experimental import pallas as pl
from jax.experimental.pallas import tpu as pltpu
from jax.sharding import PartitionSpec as P

MESH = pl.DeviceIdType.MESH
F32, BF16 = jnp.float32, jnp.bfloat16
M = 128
NX, NY, NZ = 2, 8, 10
CELLS = NX * NY * NZ
HALF = M // 2
ROWS = HALF * M
CX, CY, CZH, CZL = 4, 4, 2, 4
CZ = CZH * CZL
VMEM = pl.BlockSpec(memory_space=pltpu.VMEM)


def coords():
    s, p = lax.axis_index("stream"), lax.axis_index("span")
    core = lax.rem(s, 2)
    zh = lax.rem(s // 2, CZH)
    y = s // (2 * CZH)
    zl = p // CX
    x = lax.rem(p, CX)
    return x, y, zh * CZL + zl, core


def device(x, y, z, core):
    return ((y * CZH + z // CZL) * 2 + core, lax.rem(z, CZL) * CX + x)


def halo_kernel(phi_ref, w_ref, x_ref, halo, ext, send_sem, recv_sem):
    s, p = lax.axis_index("stream"), lax.axis_index("span")
    ns, np_ = lax.axis_size("stream"), lax.axis_size("span")
    core = lax.rem(s, 2)
    partner = (s + 1 - 2 * core, p)
    before, after = (lax.rem(s + ns - 1, ns), p), (lax.rem(s + 1, ns), p)
    left, right = (s, lax.rem(p + np_ - 1, np_)), (s, lax.rem(p + 1, np_))

    barrier = pltpu.get_barrier_semaphore()
    for peer in (before, after, left, right):
        pl.semaphore_signal(barrier, inc=1, device_id=peer, device_id_type=MESH)
    pl.semaphore_wait(barrier, 4)

    copies = []
    for slot, peer in ((1, before), (0, after), (3, left), (2, right)):
        copy = pltpu.make_async_remote_copy(
            src_ref=phi_ref,
            dst_ref=halo.at[slot],
            send_sem=send_sem.at[slot],
            recv_sem=recv_sem.at[slot],
            device_id=peer,
            device_id_type=MESH,
        )
        copy.start()
        copies.append(copy)
    from_after, from_before, from_right, from_left = copies[0], copies[1], copies[2], copies[3]

    def weight(x, z):
        return jnp.broadcast_to(w_ref[x, :, z : z + 1], (NY, M))

    def rows(x, z):
        return pl.ds((x * NZ + z) * NY, NY)

    zero = jnp.zeros((NY, M), F32)

    def own(x, z, b):
        return phi_ref[x, z, b].astype(F32)

    for x in range(NX):
        for z in range(NZ):
            for b in range(3):
                x_ref[b, core, rows(x, z), :] = phi_ref[x, z, b]
                up = own(x, z + 1, b) if z + 1 < NZ else zero
                down = own(x, z - 1, b) if z > 0 else zero
                grad = 0.5 * (up - down) * weight(x, z)
                x_ref[9 + b, core, rows(x, z), :] = grad.astype(BF16)

    from_left.wait()
    from_right.wait()
    has_left = (p > 0).astype(F32)
    has_right = (p < np_ - 1).astype(F32)
    for x in range(NX):
        for z in range(NZ):
            for b in range(3):
                ext[0:NY] = halo[2, x, z, b].astype(F32) * has_left
                ext[NY : 2 * NY] = own(x, z, b)
                ext[2 * NY : 3 * NY] = halo[3, x, z, b].astype(F32) * has_right
                near = ext[NY + 1 : 2 * NY + 1] - ext[NY - 1 : 2 * NY - 1]
                far = ext[NY + 2 : 2 * NY + 2] - ext[NY - 2 : 2 * NY - 2]
                grad = (8.0 * near - far) * (weight(x, z) * (1.0 / 12.0))
                x_ref[6 + b, core, rows(x, z), :] = grad.astype(BF16)

    def to_partner(k, first, count):
        copy = pltpu.make_async_remote_copy(
            src_ref=x_ref.at[pl.ds(first, count), core],
            dst_ref=x_ref.at[pl.ds(first, count), core],
            send_sem=send_sem.at[k],
            recv_sem=recv_sem.at[k],
            device_id=partner,
            device_id_type=MESH,
        )
        copy.start()
        return copy

    pair = [to_partner(4, 0, 3), to_partner(5, 6, 6)]

    from_before.wait()
    from_after.wait()
    has_before = (s > 0).astype(F32)
    has_after = (s < ns - 1).astype(F32)
    for z in range(NZ):
        for b in range(3):
            a0 = halo[0, 0, z, b].astype(F32) * has_before
            a1 = halo[0, 1, z, b].astype(F32) * has_before
            c0, c1 = own(0, z, b), own(1, z, b)
            d0 = halo[1, 0, z, b].astype(F32) * has_after
            d1 = halo[1, 1, z, b].astype(F32) * has_after
            g0 = (8.0 * (c1 - a1) - (d0 - a0)) * (weight(0, z) * (1.0 / 12.0))
            g1 = (8.0 * (d0 - c0) - (d1 - a1)) * (weight(1, z) * (1.0 / 12.0))
            x_ref[3 + b, core, rows(0, z), :] = g0.astype(BF16)
            x_ref[3 + b, core, rows(1, z), :] = g1.astype(BF16)
    pair.append(to_partner(6, 3, 3))
    for copy in pair:
        copy.wait()


def halo_call(phi, weight):
    return pl.pallas_call(
        halo_kernel,
        out_shape=jax.ShapeDtypeStruct((12, 2, CELLS, M), BF16),
        in_specs=[VMEM, VMEM],
        out_specs=VMEM,
        scratch_shapes=[
            pltpu.VMEM((4, NX, NZ, 3, NY, M), BF16),
            pltpu.VMEM((3 * NY, M), F32),
            pltpu.SemaphoreType.DMA((7,)),
            pltpu.SemaphoreType.DMA((7,)),
        ],
        compiler_params=pltpu.CompilerParams(
            collective_id=0, has_side_effects=True, vmem_limit_bytes=16 * 2**20
        ),
        name="halo",
    )(phi, weight)


BLOCK = 4
TILES = 8
PACK = 16
CHUNKS = (16, 16, 16, 16)
ORDER = (
    (-1, 0), (0, 0), (-1, 1), (0, 1), (-1, 2), (1, 0), (0, 2), (-1, 3), (1, 1), (0, 3), (1, 2), (2, 0),
    (1, 3), (2, 1), (3, 0), (2, 2), (3, 1), (2, 3), (3, 2), (4, 0), (3, 3), (4, 1), (5, 0), (4, 2),
    (6, 0), (5, 1), (4, 3), (5, 2), (6, 1), (6, 2), (5, 3), (6, 3),
)
COPIES = 3 + 7 + 3 + 7 + 3 + 1


def tensor_kernel(
    x_ref, full_ref, part, got1, sum1, got2, shard, phi_t, grad, test, quad_a, quad_b, send_sem, recv_sem
):
    x, y, z, core = coords()
    u = x * (1 - core) + y * core
    v = y * (1 - core) + x * core

    def along_u(d):
        return device(lax.rem(x + d * (1 - core), CX), lax.rem(y + d * core, CY), z, core)

    def along_v(d):
        return device(lax.rem(x + d * core, CX), lax.rem(y + d * (1 - core), CY), z, core)

    def along_z(d):
        return device(x, y, lax.rem(z + d, CZ), core)

    partner = device(x, y, z, 1 - core)
    barrier = pltpu.get_barrier_semaphore()
    peers = [along_u(d) for d in (1, 2, 3)] + [along_v(d) for d in (1, 2, 3)]
    peers += [along_z(d) for d in range(1, CZ)] + [partner]
    for peer in peers:
        pl.semaphore_signal(barrier, inc=1, device_id=peer, device_id_type=MESH)


    def piece(q, first, count):
        dev, row = first // CELLS, first % CELLS
        if row + count <= CELLS:
            return x_ref[q, dev, row : row + count, :]
        head = CELLS - row
        return jnp.concatenate(
            [x_ref[q, dev, row:CELLS, :], x_ref[q, dev + 1, 0 : count - head, :]], axis=0
        )

    def tile(base, stride, t):
        if t < 6:
            return piece(base + stride * (t // 2), (t % 2) * M, M)
        if t == 6:
            return jnp.concatenate(
                [piece(base, 2 * M, 64), piece(base + stride, 2 * M, 64)], axis=0
            )
        return jnp.concatenate(
            [piece(base + 2 * stride, 2 * M, 64), jnp.zeros((64, M), BF16)], axis=0
        )

    for t in range(TILES):
        test[t * M // PACK : (t + 1) * M // PACK] = tile(0, 1, t).reshape(M // PACK, PACK, M)
        for b in range(3):
            grad[b, t] = tile(3 + b, 3, t).astype(F32).T
    for b in range(3):
        for half in range(3):
            if half < 2:
                cells = piece(b, half * M, M)
            else:
                tail = piece(b, 2 * M, 64)
                cells = jnp.concatenate([tail, tail], axis=0)
            phi_t[b, half] = cells.astype(F32).T

    def quads(block, quad):
        first = core * HALF + block * BLOCK

        def row(n, b, half):
            wide = jnp.broadcast_to(phi_t[b, half, pl.ds(first + n, 1), :], (PACK, M))
            return wide.astype(BF16)

        for t in range(TILES):
            half = t % 2 if t < 6 else 2
            phi = [[row(n, b, half) for b in range(3)] for n in range(BLOCK)]
            for k in range(0, M, PACK):
                g = [grad[b, t, k : k + PACK, :].astype(BF16) for b in range(3)]
                for n in range(BLOCK):
                    q = phi[n][0] * g[0] + phi[n][1] * g[1] + phi[n][2] * g[2]
                    quad[t, (n * M + k) // PACK] = q

    def contract(block, quad):
        left = jnp.concatenate([quad[t].reshape(BLOCK * M, M) for t in range(TILES)], axis=1)
        res = jnp.dot(left, test[...].reshape(TILES * M, M), preferred_element_type=F32)
        for n in range(BLOCK):
            first = pl.multiple_of((block * BLOCK + n) * M, M)
            part[pl.ds(first, M), :] = res[n * M : (n + 1) * M].T.astype(BF16)

    def two_blocks(turn, more):
        quads(2 * turn + 1, quad_b)
        contract(2 * turn, quad_a)
        if more:
            quads(2 * turn + 2, quad_a)
        contract(2 * turn + 1, quad_b)

    starts = [sum(CHUNKS[:c]) for c in range(len(CHUNKS))]

    def compute(c):
        last = c == len(CHUNKS) - 1
        begin, end = starts[c] // (2 * BLOCK), (starts[c] + CHUNKS[c]) // (2 * BLOCK)
        if c == 0:
            quads(0, quad_a)

        @pl.loop(begin, end - 1 if last else end)
        def _(turn):
            two_blocks(turn, True)

        if last:
            two_blocks(end - 1, False)


    flying = {}

    def send(c, k, src, dst, peer):
        copy = pltpu.make_async_remote_copy(
            src_ref=src,
            dst_ref=dst,
            send_sem=send_sem.at[c, k],
            recv_sem=recv_sem.at[c, k],
            device_id=peer,
            device_id_type=MESH,
        )
        copy.start()
        flying.setdefault(c, []).append(copy)

    def wait(c):
        for copy in flying.pop(c):
            copy.wait()

    def rows(first, count):
        return pl.ds(pl.multiple_of(first, count), count)

    def at1(c):
        return starts[c] * M // 4

    def at2(c):
        return starts[c] * M // 32

    def stage(k, c):
        n0 = CHUNKS[c] * M
        n1, n2 = n0 // 4, n0 // 32
        first = starts[c] * M
        part_row = lambda uu: pl.ds(pl.multiple_of(first + uu * n1, n2), n1)
        full_row = lambda uu, zz: pl.ds(pl.multiple_of(first + uu * n1 + zz * n2, n2), n2)
        if k > 0:
            wait(c)
        if k == 0:
            for d in (2, 1, 3):
                there = lax.rem(u + d, 4)
                send(c, d - 1, part.at[part_row(there)], got1.at[d - 1, pl.ds(at1(c), n1)], along_u(d))
        if k == 1:
            total = part[part_row(u), :].astype(F32)
            for d in range(3):
                total = total + got1[d, at1(c) : at1(c) + n1, :].astype(F32)
            sum1[at1(c) : at1(c) + n1, :] = total.astype(BF16)
            for d in (4, 3, 5, 2, 6, 1, 7):
                there = lax.rem(z + d, CZ)
                send(
                    c, 2 + d,
                    sum1.at[pl.ds(pl.multiple_of(at1(c) + there * n2, n2), n2)],
                    got2.at[d - 1, pl.ds(at2(c), n2)],
                    along_z(d),
                )
        if k == 2:
            total = sum1[pl.ds(pl.multiple_of(at1(c) + z * n2, n2), n2), :].astype(F32)
            for d in range(CZ - 1):
                total = total + got2[d, at2(c) : at2(c) + n2, :].astype(F32)
            shard[v, at2(c) : at2(c) + n2, :] = total.astype(BF16)
            mine = shard.at[v, pl.ds(at2(c), n2)]
            for d in (2, 1, 3):
                send(c, 9 + d, mine, mine, along_v(d))
        if k == 3:
            total = shard[0, at2(c) : at2(c) + n2, :].astype(F32)
            for d in range(1, 4):
                total = total + shard[d, at2(c) : at2(c) + n2, :].astype(F32)
            full_ref[core, full_row(u, z), :] = total.astype(BF16)
            mine = full_ref.at[core, full_row(u, z)]
            for d in (4, 3, 5, 2, 6, 1, 7):
                send(c, 12 + d, mine, mine, along_z(d))
        if k == 4:
            mine = full_ref.at[core, part_row(u)]
            for d in (2, 1, 3):
                send(c, 19 + d, mine, mine, along_u(d))
        if k == 5:
            mine = full_ref.at[core, pl.ds(first, n0)]
            send(c, 23, mine, mine, partner)

    for k, c in ORDER:
        if k < 0:
            compute(c)
            if c == 0:
                pl.semaphore_wait(barrier, len(peers))
        else:
            stage(k, c)


def tensor_call(gathered):
    return pl.pallas_call(
        tensor_kernel,
        out_shape=jax.ShapeDtypeStruct((2, ROWS, M), BF16),
        in_specs=[VMEM],
        out_specs=VMEM,
        scratch_shapes=[
            pltpu.VMEM((ROWS, M), BF16),
            pltpu.VMEM((3, ROWS // 4, M), BF16),
            pltpu.VMEM((ROWS // 4, M), BF16),
            pltpu.VMEM((CZ - 1, ROWS // 32, M), BF16),
            pltpu.VMEM((4, ROWS // 32, M), BF16),
            pltpu.VMEM((3, 3, M, M), F32),
            pltpu.VMEM((3, TILES, M, M), F32),
            pltpu.VMEM((TILES * M // PACK, PACK, M), BF16),
            pltpu.VMEM((TILES, BLOCK * M // PACK, PACK, M), BF16),
            pltpu.VMEM((TILES, BLOCK * M // PACK, PACK, M), BF16),
            pltpu.SemaphoreType.DMA((len(CHUNKS), COPIES)),
            pltpu.SemaphoreType.DMA((len(CHUNKS), COPIES)),
        ],
        compiler_params=pltpu.CompilerParams(
            collective_id=1, has_side_effects=True, vmem_limit_bytes=32 * 2**20
        ),
        name="tensor",
    )(gathered)


def shards(velocity_modes, cell_weight):
    phi = jnp.transpose(velocity_modes, (0, 2, 3, 1, 4))
    gathered = halo_call(phi, cell_weight)
    full = tensor_call(gathered)
    return full.reshape(M, M, M).astype(F32)


def solution(mesh):
    placed = (P("stream", "span", None, None, None), P("stream", "span", None))
    return jax.shard_map(shards, mesh=mesh, in_specs=placed, out_specs=P(), check_vma=False)
```

```python
import jax
import jax.numpy as jnp
from jax import lax
from jax.experimental import pallas as pl
from jax.experimental.pallas import tpu as pltpu
from jax.sharding import PartitionSpec as P

MESH = pl.DeviceIdType.MESH
F32, BF16 = jnp.float32, jnp.bfloat16
M = 128
NX, NY, NZ = 2, 8, 10
CELLS = NX * NY * NZ
HALF = M // 2
ROWS = HALF * M
CX, CY, CZH, CZL = 4, 4, 2, 4
CZ = CZH * CZL
VMEM = pl.BlockSpec(memory_space=pltpu.VMEM)


def coords():
    s, p = lax.axis_index("stream"), lax.axis_index("span")
    core = lax.rem(s, 2)
    zh = lax.rem(s // 2, CZH)
    y = s // (2 * CZH)
    zl = p // CX
    x = lax.rem(p, CX)
    return x, y, zh * CZL + zl, core


def device(x, y, z, core):
    return ((y * CZH + z // CZL) * 2 + core, lax.rem(z, CZL) * CX + x)


BLOCK = 4
PACK = 16
TILES_YZ, TILES_X = 5, 3
TILES = TILES_YZ + TILES_X
CHUNKS = (16, 16, 16, 16)
ORDER = (
    (-1, 0), (0, 0), (-1, 1), (0, 1), (-1, 2), (1, 0), (0, 2), (-1, 3), (1, 1), (0, 3), (1, 2), (2, 0),
    (1, 3), (2, 1), (3, 0), (2, 2), (3, 1), (2, 3), (3, 2), (4, 0), (3, 3), (4, 1), (5, 0), (4, 2),
    (6, 0), (4, 3), (5, 1), (5, 2), (6, 1), (5, 3), (6, 2), (6, 3),
)
COPIES = 3 + 7 + 3 + 7 + 3 + 4
FAR = 2


def tensor_kernel(
    phi_hbm, w_hbm, full_ref, own, w_ref, halo, ext, xs, part, got1, sum1, got2, shard,
    phi_t, grad, test, quad_a, quad_b, local_sem, halo_send, halo_recv, send_sem, recv_sem,
):
    s, p = lax.axis_index("stream"), lax.axis_index("span")
    ns, np_ = lax.axis_size("stream"), lax.axis_size("span")
    before, after = (lax.rem(s + ns - 1, ns), p), (lax.rem(s + 1, ns), p)
    left, right = (s, lax.rem(p + np_ - 1, np_)), (s, lax.rem(p + 1, np_))
    x, y, z, core = coords()
    u = x * (1 - core) + y * core
    v = y * (1 - core) + x * core

    def along_u(d):
        return device(lax.rem(x + d * (1 - core), CX), lax.rem(y + d * core, CY), z, core)

    def along_v(d):
        return device(lax.rem(x + d * core, CX), lax.rem(y + d * (1 - core), CY), z, core)

    def along_z(d):
        return device(x, y, lax.rem(z + d, CZ), core)

    partner = device(x, y, z, 1 - core)
    barrier = pltpu.get_barrier_semaphore()
    peers = [before, after, left, right, partner]
    peers += [along_u(d) for d in (1, 2, 3)] + [along_v(d) for d in (1, 2, 3)]
    peers += [along_z(d) for d in range(1, CZ)]
    for peer in peers:
        pl.semaphore_signal(barrier, inc=1, device_id=peer, device_id_type=MESH)
    take = [
        pltpu.make_async_copy(phi_hbm, own, local_sem.at[0]),
        pltpu.make_async_copy(w_hbm, w_ref, local_sem.at[1]),
    ]
    for copy in take:
        copy.start()
    pl.semaphore_wait(barrier, len(peers))


    def halo_copy(k, src, dst, peer):
        copy = pltpu.make_async_remote_copy(
            src_ref=src,
            dst_ref=dst,
            send_sem=halo_send.at[k],
            recv_sem=halo_recv.at[k],
            device_id=peer,
            device_id_type=MESH,
        )
        copy.start()
        return copy

    far_halo = []
    for n in range(FAR):
        zs = pl.ds(n * NZ // FAR, NZ // FAR)
        far_halo.append(
            (
                halo_copy(7 + n, phi_hbm.at[:, zs], halo.at[1, :, zs], before),
                halo_copy(7 + FAR + n, phi_hbm.at[:, zs], halo.at[0, :, zs], after),
            )
        )
    from_right = halo_copy(3, phi_hbm, halo.at[3], left)
    from_left = halo_copy(2, phi_hbm, halo.at[2], right)
    for copy in take:
        copy.wait()

    def weight(x, z):
        return jnp.broadcast_to(w_ref[x, :, z : z + 1], (NY, M))

    def cells_at(x, z):
        return pl.ds((x * NZ + z) * NY, NY)

    def here(x, z, b):
        return own[x, z, b].astype(F32)

    def to_partner(k, first, count):
        mine = xs.at[pl.ds(first, count), core]
        return halo_copy(k, mine, mine, partner)

    zero = jnp.zeros((NY, M), F32)
    for x_ in range(NX):
        for z_ in range(NZ):
            for b in range(3):
                xs[b, core, cells_at(x_, z_), :] = own[x_, z_, b]
                up = here(x_, z_ + 1, b) if z_ + 1 < NZ else zero
                down = here(x_, z_ - 1, b) if z_ > 0 else zero
                g = 0.5 * (up - down) * weight(x_, z_)
                xs[9 + b, core, cells_at(x_, z_), :] = g.astype(BF16)
    pair = [to_partner(4, 0, 3), to_partner(5, 9, 3)]

    from_left.wait()
    from_right.wait()
    has_left = (p > 0).astype(F32)
    has_right = (p < np_ - 1).astype(F32)
    for x_ in range(NX):
        for z_ in range(NZ):
            for b in range(3):
                line = ext.at[(x_ * NZ + z_) * 3 + b]
                line[0:NY] = halo[2, x_, z_, b].astype(F32) * has_left
                line[NY : 2 * NY] = here(x_, z_, b)
                line[2 * NY : 3 * NY] = halo[3, x_, z_, b].astype(F32) * has_right
    for x_ in range(NX):
        for z_ in range(NZ):
            for b in range(3):
                line = ext.at[(x_ * NZ + z_) * 3 + b]
                near = line[NY + 1 : 2 * NY + 1] - line[NY - 1 : 2 * NY - 1]
                far = line[NY + 2 : 2 * NY + 2] - line[NY - 2 : 2 * NY - 2]
                g = (8.0 * near - far) * (weight(x_, z_) * (1.0 / 12.0))
                xs[6 + b, core, cells_at(x_, z_), :] = g.astype(BF16)
    pair.append(to_partner(6, 6, 3))
    for copy in pair:
        copy.wait()


    def piece(q, first, count):
        dev, row = first // CELLS, first % CELLS
        if row + count <= CELLS:
            return xs[q, dev, row : row + count, :]
        head = CELLS - row
        return jnp.concatenate(
            [xs[q, dev, row:CELLS, :], xs[q, dev + 1, 0 : count - head, :]], axis=0
        )

    def tile(qx, qy, qz, t):
        if t < 4:
            return piece((qy, qz)[t // 2], (t % 2) * M, M)
        if t == 4:
            return jnp.concatenate([piece(qy, 2 * M, 64), piece(qz, 2 * M, 64)], axis=0)
        if t < 7:
            return piece(qx, (t - 5) * M, M)
        return jnp.concatenate([piece(qx, 2 * M, 64), jnp.zeros((64, M), BF16)], axis=0)

    HALVES = (0, 1, 0, 1, 2, 0, 1, 2)

    def load_grad(t):
        for b in range(3):
            grad[b, t] = tile(3 + b, 6 + b, 9 + b, t).astype(F32).T

    for t in range(TILES):
        test[t * M // PACK : (t + 1) * M // PACK] = tile(0, 1, 2, t).reshape(M // PACK, PACK, M)
    for b in range(3):
        for half in range(3):
            if half < 2:
                cells = piece(b, half * M, M)
            else:
                tail = piece(b, 2 * M, 64)
                cells = jnp.concatenate([tail, tail], axis=0)
            phi_t[b, half] = cells.astype(F32).T
    for t in range(TILES_YZ):
        load_grad(t)


    has_before = (s > 0).astype(F32)
    has_after = (s < ns - 1).astype(F32)
    pair = []
    for n in range(FAR):
        for copy in far_halo[n]:
            copy.wait()
        zs = range(n * NZ // FAR, (n + 1) * NZ // FAR)
        for z_ in zs:
            for b in range(3):
                a0 = halo[0, 0, z_, b].astype(F32) * has_before
                a1 = halo[0, 1, z_, b].astype(F32) * has_before
                c0, c1 = here(0, z_, b), here(1, z_, b)
                d0 = halo[1, 0, z_, b].astype(F32) * has_after
                d1 = halo[1, 1, z_, b].astype(F32) * has_after
                g0 = (8.0 * (c1 - a1) - (d0 - a0)) * (weight(0, z_) * (1.0 / 12.0))
                g1 = (8.0 * (d0 - c0) - (d1 - a1)) * (weight(1, z_) * (1.0 / 12.0))
                xs[3 + b, core, cells_at(0, z_), :] = g0.astype(BF16)
                xs[3 + b, core, cells_at(1, z_), :] = g1.astype(BF16)
        for x_ in range(NX):
            mine = xs.at[pl.ds(3, 3), core, pl.ds((x_ * NZ + zs[0]) * NY, len(zs) * NY)]
            pair.append(halo_copy(7 + 2 * FAR + n * NX + x_, mine, mine, partner))
    for copy in pair:
        copy.wait()
    for t in range(TILES_YZ, TILES):
        load_grad(t)

    def quads(block, quad):
        first = core * HALF + block * BLOCK

        def row(n, b, half):
            wide = jnp.broadcast_to(phi_t[b, half, pl.ds(first + n, 1), :], (PACK, M))
            return wide.astype(BF16)

        for t in range(TILES):
            phi = [[row(n, b, HALVES[t]) for b in range(3)] for n in range(BLOCK)]
            for k in range(0, M, PACK):
                g = [grad[b, t, k : k + PACK, :].astype(BF16) for b in range(3)]
                for n in range(BLOCK):
                    q = phi[n][0] * g[0] + phi[n][1] * g[1] + phi[n][2] * g[2]
                    quad[t, (n * M + k) // PACK] = q

    def contract(block, quad):
        wide = jnp.concatenate([quad[t].reshape(BLOCK * M, M) for t in range(TILES)], axis=1)
        res = jnp.dot(wide, test[...].reshape(TILES * M, M), preferred_element_type=F32)
        for n in range(BLOCK):
            first = pl.multiple_of((block * BLOCK + n) * M, M)
            part[pl.ds(first, M), :] = res[n * M : (n + 1) * M].T.astype(BF16)

    def two_blocks(turn, more):
        quads(2 * turn + 1, quad_b)
        contract(2 * turn, quad_a)
        if more:
            quads(2 * turn + 2, quad_a)
        contract(2 * turn + 1, quad_b)

    turns = HALF // (2 * BLOCK)
    starts = [sum(CHUNKS[:c]) for c in range(len(CHUNKS))]

    def compute(c):
        last = c == len(CHUNKS) - 1
        begin, end = starts[c] // (2 * BLOCK), (starts[c] + CHUNKS[c]) // (2 * BLOCK)
        if c == 0:
            quads(0, quad_a)

        @pl.loop(begin, end - 1 if last else end)
        def _(turn):
            two_blocks(turn, True)

        if last:
            two_blocks(turns - 1, False)


    flying = {}

    def send(c, k, src, dst, peer):
        copy = pltpu.make_async_remote_copy(
            src_ref=src,
            dst_ref=dst,
            send_sem=send_sem.at[c, k],
            recv_sem=recv_sem.at[c, k],
            device_id=peer,
            device_id_type=MESH,
        )
        copy.start()
        flying.setdefault(c, []).append(copy)

    def wait(c):
        for copy in flying.pop(c):
            copy.wait()

    def at1(c):
        return starts[c] * M // 4

    def at2(c):
        return starts[c] * M // 32

    def stage(k, c):
        n0 = CHUNKS[c] * M
        n1, n2 = n0 // 4, n0 // 32
        first = starts[c] * M
        part_row = lambda uu: pl.ds(pl.multiple_of(first + uu * n1, n2), n1)
        full_row = lambda uu, zz: pl.ds(pl.multiple_of(first + uu * n1 + zz * n2, n2), n2)
        if k > 0 and k != 5:
            wait(c)
        if k == 0:
            for d in (2, 1, 3):
                there = lax.rem(u + d, 4)
                send(c, d - 1, part.at[part_row(there)], got1.at[d - 1, pl.ds(at1(c), n1)], along_u(d))
        if k == 1:
            total = part[part_row(u), :].astype(F32)
            for d in range(3):
                total = total + got1[d, at1(c) : at1(c) + n1, :].astype(F32)
            sum1[at1(c) : at1(c) + n1, :] = total.astype(BF16)
            for d in (4, 3, 5, 2, 6, 1, 7):
                there = lax.rem(z + d, CZ)
                send(
                    c, 2 + d,
                    sum1.at[pl.ds(pl.multiple_of(at1(c) + there * n2, n2), n2)],
                    got2.at[d - 1, pl.ds(at2(c), n2)],
                    along_z(d),
                )
        if k == 2:
            total = sum1[pl.ds(pl.multiple_of(at1(c) + z * n2, n2), n2), :].astype(F32)
            for d in range(CZ - 1):
                total = total + got2[d, at2(c) : at2(c) + n2, :].astype(F32)
            shard[v, at2(c) : at2(c) + n2, :] = total
            mine = shard.at[v, pl.ds(at2(c), n2)]
            for d in (2, 1, 3):
                send(c, 9 + d, mine, mine, along_v(d))
        if k == 3:
            total = shard[0, at2(c) : at2(c) + n2, :]
            for d in range(1, 4):
                total = total + shard[d, at2(c) : at2(c) + n2, :]
            full_ref[core, full_row(u, z), :] = total.astype(BF16)
            mine = full_ref.at[core, full_row(u, z)]
            for d in (4, 3, 5, 2, 6, 1, 7):
                send(c, 12 + d, mine, mine, along_z(d))
        if k == 4:
            mine = full_ref.at[core, part_row(u)]
            for d in (2, 1, 3):
                send(c, 19 + d, mine, mine, along_u(d))
            send(c, 23, mine, mine, partner)
        if k == 5:
            two, one, three, own_piece = flying.pop(c)
            for d, copy in ((1, one), (3, three), (2, two)):
                copy.wait()
                piece_u = full_ref.at[core, part_row(lax.rem(u + 4 - d, 4))]
                send(c, 23 + d, piece_u, piece_u, partner)
            flying[c].append(own_piece)

    for k, c in ORDER:
        if k < 0:
            compute(c)
        else:
            stage(k, c)


def tensor_call(phi, weight):
    return pl.pallas_call(
        tensor_kernel,
        out_shape=jax.ShapeDtypeStruct((2, ROWS, M), BF16),
        in_specs=[pl.BlockSpec(memory_space=pltpu.MemorySpace.HBM)] * 2,
        out_specs=VMEM,
        scratch_shapes=[
            pltpu.VMEM((NX, NZ, 3, NY, M), BF16),
            pltpu.VMEM((NX, NY, NZ), F32),
            pltpu.VMEM((4, NX, NZ, 3, NY, M), BF16),
            pltpu.VMEM((NX * NZ * 3, 3 * NY, M), F32),
            pltpu.VMEM((12, 2, CELLS, M), BF16),
            pltpu.VMEM((ROWS, M), BF16),
            pltpu.VMEM((3, ROWS // 4, M), BF16),
            pltpu.VMEM((ROWS // 4, M), BF16),
            pltpu.VMEM((CZ - 1, ROWS // 32, M), BF16),
            pltpu.VMEM((4, ROWS // 32, M), F32),
            pltpu.VMEM((3, 3, M, M), F32),
            pltpu.VMEM((3, TILES, M, M), F32),
            pltpu.VMEM((TILES * M // PACK, PACK, M), BF16),
            pltpu.VMEM((TILES, BLOCK * M // PACK, PACK, M), BF16),
            pltpu.VMEM((TILES, BLOCK * M // PACK, PACK, M), BF16),
            pltpu.SemaphoreType.DMA((2,)),
            pltpu.SemaphoreType.DMA((7 + 4 * FAR,)),
            pltpu.SemaphoreType.DMA((7 + 4 * FAR,)),
            pltpu.SemaphoreType.DMA((len(CHUNKS), COPIES)),
            pltpu.SemaphoreType.DMA((len(CHUNKS), COPIES)),
        ],
        compiler_params=pltpu.CompilerParams(
            collective_id=0, has_side_effects=True, vmem_limit_bytes=40 * 2**20
        ),
        name="tensor",
    )(pltpu.with_memory_space_constraint(phi, pltpu.HBM), pltpu.with_memory_space_constraint(weight, pltpu.HBM))


PARTS = 16


def widen_kernel(src_ref, out_ref, wide, sem):
    count = M * M // PARTS
    copies = []
    for n in range(PARTS):
        wide[n * count : (n + 1) * count, :] = src_ref[n * count : (n + 1) * count, :].astype(F32)
        span = pl.ds(n * count, count)
        copy = pltpu.make_async_copy(wide.at[span], out_ref.at[span], sem.at[n])
        copy.start()
        copies.append(copy)
    for copy in copies:
        copy.wait()


def widen_call(full):
    return pl.pallas_call(
        widen_kernel,
        out_shape=jax.ShapeDtypeStruct((M * M, M), F32),
        in_specs=[VMEM],
        out_specs=pl.BlockSpec(memory_space=pl.ANY),
        scratch_shapes=[pltpu.VMEM((M * M, M), F32), pltpu.SemaphoreType.DMA((PARTS,))],
        compiler_params=pltpu.CompilerParams(vmem_limit_bytes=24 * 2**20),
        name="widen",
    )(full)


def shards(velocity_modes, cell_weight):
    phi = jnp.transpose(velocity_modes, (0, 2, 3, 1, 4))
    full = tensor_call(phi, cell_weight)
    return widen_call(full.reshape(M * M, M)).reshape(M, M, M)


def solution(mesh):
    placed = (P("stream", "span", None, None, None), P("stream", "span", None))
    return jax.shard_map(shards, mesh=mesh, in_specs=placed, out_specs=P(), check_vma=False)
```

```python
import jax
import jax.numpy as jnp
from jax import lax
from jax.experimental import pallas as pl
from jax.experimental.pallas import tpu as pltpu
from jax.sharding import PartitionSpec as P

MESH = pl.DeviceIdType.MESH
F32, BF16 = jnp.float32, jnp.bfloat16
M = 128
NX, NY, NZ = 2, 8, 10
CELLS = NX * NY * NZ
HALF = M // 2
ROWS = HALF * M
CX, CY, CZH, CZL = 4, 4, 2, 4
CZ = CZH * CZL
VMEM = pl.BlockSpec(memory_space=pltpu.VMEM)


def coords():
    s, p = lax.axis_index("stream"), lax.axis_index("span")
    core = lax.rem(s, 2)
    zh = lax.rem(s // 2, CZH)
    y = s // (2 * CZH)
    zl = p // CX
    x = lax.rem(p, CX)
    return x, y, zh * CZL + zl, core


def device(x, y, z, core):
    return ((y * CZH + z // CZL) * 2 + core, lax.rem(z, CZL) * CX + x)


BLOCK = 4
PACK = 16
TILES_YZ, TILES_X = 5, 3
TILES = TILES_YZ + TILES_X
CHUNKS = (16, 16, 16, 16)
ORDER = (
    (-1, 0), (0, 0), (-1, 1), (0, 1), (-1, 2), (0, 2), (1, 0), (-1, 3), (0, 3), (1, 1), (1, 2), (2, 0),
    (1, 3), (2, 1), (3, 0), (2, 2), (3, 1), (2, 3), (3, 2), (4, 0), (3, 3), (4, 1), (4, 2), (4, 3),
    (5, 0), (5, 2), (5, 1), (5, 3), (6, 0), (6, 1), (6, 2), (6, 3),
)
COPIES = 3 + 7 + 3 + 7 + 3 + 4
FAR = 2


def tensor_kernel(
    phi_hbm, w_hbm, full_ref, own, w_ref, halo, ext, xs, part, got1, sum1, got2, shard,
    phi_t, grad, test, quad_a, quad_b, local_sem, halo_send, halo_recv, send_sem, recv_sem,
):
    s, p = lax.axis_index("stream"), lax.axis_index("span")
    ns, np_ = lax.axis_size("stream"), lax.axis_size("span")
    before, after = (lax.rem(s + ns - 1, ns), p), (lax.rem(s + 1, ns), p)
    left, right = (s, lax.rem(p + np_ - 1, np_)), (s, lax.rem(p + 1, np_))
    x, y, z, core = coords()
    u = x * (1 - core) + y * core
    v = y * (1 - core) + x * core

    def along_u(d):
        return device(lax.rem(x + d * (1 - core), CX), lax.rem(y + d * core, CY), z, core)

    def along_v(d):
        return device(lax.rem(x + d * core, CX), lax.rem(y + d * (1 - core), CY), z, core)

    def along_z(d):
        return device(x, y, lax.rem(z + d, CZ), core)

    partner = device(x, y, z, 1 - core)
    barrier = pltpu.get_barrier_semaphore()
    peers = [before, after, left, right, partner]
    peers += [along_u(d) for d in (1, 2, 3)] + [along_v(d) for d in (1, 2, 3)]
    peers += [along_z(d) for d in range(1, CZ)]
    for peer in peers:
        pl.semaphore_signal(barrier, inc=1, device_id=peer, device_id_type=MESH)
    take = [
        pltpu.make_async_copy(phi_hbm, own, local_sem.at[0]),
        pltpu.make_async_copy(w_hbm, w_ref, local_sem.at[1]),
    ]
    for copy in take:
        copy.start()
    pl.semaphore_wait(barrier, len(peers))


    def halo_copy(k, src, dst, peer):
        copy = pltpu.make_async_remote_copy(
            src_ref=src,
            dst_ref=dst,
            send_sem=halo_send.at[k],
            recv_sem=halo_recv.at[k],
            device_id=peer,
            device_id_type=MESH,
        )
        copy.start()
        return copy

    far_halo = []
    for n in range(FAR):
        zs = pl.ds(n * NZ // FAR, NZ // FAR)
        far_halo.append(
            (
                halo_copy(7 + n, phi_hbm.at[:, zs], halo.at[1, :, zs], before),
                halo_copy(7 + FAR + n, phi_hbm.at[:, zs], halo.at[0, :, zs], after),
            )
        )
    from_right = halo_copy(3, phi_hbm, halo.at[3], left)
    from_left = halo_copy(2, phi_hbm, halo.at[2], right)
    for copy in take:
        copy.wait()

    def weight(x, z):
        return jnp.broadcast_to(w_ref[x, :, z : z + 1], (NY, M))

    def cells_at(x, z):
        return pl.ds((x * NZ + z) * NY, NY)

    def here(x, z, b):
        return own[x, z, b].astype(F32)

    def to_partner(k, first, count):
        mine = xs.at[pl.ds(first, count), core]
        return halo_copy(k, mine, mine, partner)

    zero = jnp.zeros((NY, M), F32)
    for x_ in range(NX):
        for z_ in range(NZ):
            for b in range(3):
                xs[b, core, cells_at(x_, z_), :] = own[x_, z_, b]
                up = here(x_, z_ + 1, b) if z_ + 1 < NZ else zero
                down = here(x_, z_ - 1, b) if z_ > 0 else zero
                g = 0.5 * (up - down) * weight(x_, z_)
                xs[9 + b, core, cells_at(x_, z_), :] = g.astype(BF16)
    pair = [to_partner(4, 0, 3), to_partner(5, 9, 3)]

    from_left.wait()
    from_right.wait()
    has_left = (p > 0).astype(F32)
    has_right = (p < np_ - 1).astype(F32)
    for x_ in range(NX):
        for z_ in range(NZ):
            for b in range(3):
                line = ext.at[(x_ * NZ + z_) * 3 + b]
                line[0:NY] = halo[2, x_, z_, b].astype(F32) * has_left
                line[NY : 2 * NY] = here(x_, z_, b)
                line[2 * NY : 3 * NY] = halo[3, x_, z_, b].astype(F32) * has_right
    for x_ in range(NX):
        for z_ in range(NZ):
            for b in range(3):
                line = ext.at[(x_ * NZ + z_) * 3 + b]
                near = line[NY + 1 : 2 * NY + 1] - line[NY - 1 : 2 * NY - 1]
                far = line[NY + 2 : 2 * NY + 2] - line[NY - 2 : 2 * NY - 2]
                g = (8.0 * near - far) * (weight(x_, z_) * (1.0 / 12.0))
                xs[6 + b, core, cells_at(x_, z_), :] = g.astype(BF16)
    pair.append(to_partner(6, 6, 3))
    for copy in pair:
        copy.wait()


    def piece(q, first, count):
        dev, row = first // CELLS, first % CELLS
        if row + count <= CELLS:
            return xs[q, dev, row : row + count, :]
        head = CELLS - row
        return jnp.concatenate(
            [xs[q, dev, row:CELLS, :], xs[q, dev + 1, 0 : count - head, :]], axis=0
        )

    def tile(qx, qy, qz, t):
        if t < 4:
            return piece((qy, qz)[t // 2], (t % 2) * M, M)
        if t == 4:
            return jnp.concatenate([piece(qy, 2 * M, 64), piece(qz, 2 * M, 64)], axis=0)
        if t < 7:
            return piece(qx, (t - 5) * M, M)
        return jnp.concatenate([piece(qx, 2 * M, 64), jnp.zeros((64, M), BF16)], axis=0)

    HALVES = (0, 1, 0, 1, 2, 0, 1, 2)

    def load_grad(t):
        for b in range(3):
            grad[b, t] = tile(3 + b, 6 + b, 9 + b, t).astype(F32).T

    for t in range(TILES):
        test[t * M // PACK : (t + 1) * M // PACK] = tile(0, 1, 2, t).reshape(M // PACK, PACK, M)
    for b in range(3):
        for half in range(3):
            if half < 2:
                cells = piece(b, half * M, M)
            else:
                tail = piece(b, 2 * M, 64)
                cells = jnp.concatenate([tail, tail], axis=0)
            phi_t[b, half] = cells.astype(F32).T
    for t in range(TILES_YZ):
        load_grad(t)


    has_before = (s > 0).astype(F32)
    has_after = (s < ns - 1).astype(F32)
    pair = []
    for n in range(FAR):
        for copy in far_halo[n]:
            copy.wait()
        zs = range(n * NZ // FAR, (n + 1) * NZ // FAR)
        for z_ in zs:
            for b in range(3):
                a0 = halo[0, 0, z_, b].astype(F32) * has_before
                a1 = halo[0, 1, z_, b].astype(F32) * has_before
                c0, c1 = here(0, z_, b), here(1, z_, b)
                d0 = halo[1, 0, z_, b].astype(F32) * has_after
                d1 = halo[1, 1, z_, b].astype(F32) * has_after
                g0 = (8.0 * (c1 - a1) - (d0 - a0)) * (weight(0, z_) * (1.0 / 12.0))
                g1 = (8.0 * (d0 - c0) - (d1 - a1)) * (weight(1, z_) * (1.0 / 12.0))
                xs[3 + b, core, cells_at(0, z_), :] = g0.astype(BF16)
                xs[3 + b, core, cells_at(1, z_), :] = g1.astype(BF16)
        for x_ in range(NX):
            mine = xs.at[pl.ds(3, 3), core, pl.ds((x_ * NZ + zs[0]) * NY, len(zs) * NY)]
            pair.append(halo_copy(7 + 2 * FAR + n * NX + x_, mine, mine, partner))
    for copy in pair:
        copy.wait()
    for t in range(TILES_YZ, TILES):
        load_grad(t)

    def quads(block, quad):
        first = core * HALF + block * BLOCK

        def row(n, b, half):
            wide = jnp.broadcast_to(phi_t[b, half, pl.ds(first + n, 1), :], (PACK, M))
            return wide.astype(BF16)

        for t in range(TILES):
            phi = [[row(n, b, HALVES[t]) for b in range(3)] for n in range(BLOCK)]
            for k in range(0, M, PACK):
                g = [grad[b, t, k : k + PACK, :].astype(BF16) for b in range(3)]
                for n in range(BLOCK):
                    q = phi[n][0] * g[0] + phi[n][1] * g[1] + phi[n][2] * g[2]
                    quad[t, (n * M + k) // PACK] = q

    def contract(block, quad):
        wide = jnp.concatenate([quad[t].reshape(BLOCK * M, M) for t in range(TILES)], axis=1)
        res = jnp.dot(wide, test[...].reshape(TILES * M, M), preferred_element_type=F32)
        for n in range(BLOCK):
            first = pl.multiple_of((block * BLOCK + n) * M, M)
            part[pl.ds(first, M), :] = res[n * M : (n + 1) * M].T.astype(BF16)

    def two_blocks(turn, more):
        quads(2 * turn + 1, quad_b)
        contract(2 * turn, quad_a)
        if more:
            quads(2 * turn + 2, quad_a)
        contract(2 * turn + 1, quad_b)

    turns = HALF // (2 * BLOCK)
    starts = [sum(CHUNKS[:c]) for c in range(len(CHUNKS))]

    def compute(c):
        last = c == len(CHUNKS) - 1
        begin, end = starts[c] // (2 * BLOCK), (starts[c] + CHUNKS[c]) // (2 * BLOCK)
        if c == 0:
            quads(0, quad_a)

        @pl.loop(begin, end - 1 if last else end)
        def _(turn):
            two_blocks(turn, True)

        if last:
            two_blocks(turns - 1, False)


    flying = {}

    def send(c, k, src, dst, peer):
        copy = pltpu.make_async_remote_copy(
            src_ref=src,
            dst_ref=dst,
            send_sem=send_sem.at[c, k],
            recv_sem=recv_sem.at[c, k],
            device_id=peer,
            device_id_type=MESH,
        )
        copy.start()
        flying.setdefault(c, []).append(copy)

    def wait(c):
        for copy in flying.pop(c):
            copy.wait()

    def at1(c):
        return starts[c] * M // 4

    def at2(c):
        return starts[c] * M // 32

    def stage(k, c):
        n0 = CHUNKS[c] * M
        n1, n2 = n0 // 4, n0 // 32
        first = starts[c] * M
        part_row = lambda uu: pl.ds(pl.multiple_of(first + uu * n1, n2), n1)
        full_row = lambda uu, zz: pl.ds(pl.multiple_of(first + uu * n1 + zz * n2, n2), n2)
        if k > 0 and k != 5:
            wait(c)
        if k == 0:
            for d in (2, 1, 3):
                there = lax.rem(u + d, 4)
                send(c, d - 1, part.at[part_row(there)], got1.at[d - 1, pl.ds(at1(c), n1)], along_u(d))
        if k == 1:
            total = part[part_row(u), :].astype(F32)
            for d in range(3):
                total = total + got1[d, at1(c) : at1(c) + n1, :].astype(F32)
            sum1[at1(c) : at1(c) + n1, :] = total.astype(BF16)
            for d in (4, 3, 5, 2, 6, 1, 7):
                there = lax.rem(z + d, CZ)
                send(
                    c, 2 + d,
                    sum1.at[pl.ds(pl.multiple_of(at1(c) + there * n2, n2), n2)],
                    got2.at[d - 1, pl.ds(at2(c), n2)],
                    along_z(d),
                )
        if k == 2:
            total = sum1[pl.ds(pl.multiple_of(at1(c) + z * n2, n2), n2), :].astype(F32)
            for d in range(CZ - 1):
                total = total + got2[d, at2(c) : at2(c) + n2, :].astype(F32)
            shard[v, at2(c) : at2(c) + n2, :] = total
            mine = shard.at[v, pl.ds(at2(c), n2)]
            for d in (2, 1, 3):
                send(c, 9 + d, mine, mine, along_v(d))
        if k == 3:
            total = shard[0, at2(c) : at2(c) + n2, :]
            for d in range(1, 4):
                total = total + shard[d, at2(c) : at2(c) + n2, :]
            full_ref[core, full_row(u, z), :] = total.astype(BF16)
            mine = full_ref.at[core, full_row(u, z)]
            for d in (4, 3, 5, 2, 6, 1, 7):
                send(c, 12 + d, mine, mine, along_z(d))
        if k == 4:
            mine = full_ref.at[core, part_row(u)]
            for d in (2, 1, 3):
                send(c, 19 + d, mine, mine, along_u(d))
            send(c, 23, mine, mine, partner)
        if k == 5:
            two, one, three, own_piece = flying.pop(c)
            for d, copy in ((1, one), (3, three), (2, two)):
                copy.wait()
                piece_u = full_ref.at[core, part_row(lax.rem(u + 4 - d, 4))]
                send(c, 23 + d, piece_u, piece_u, partner)
            flying[c].append(own_piece)

    for k, c in ORDER:
        if k < 0:
            compute(c)
        else:
            stage(k, c)


def tensor_call(phi, weight):
    return pl.pallas_call(
        tensor_kernel,
        out_shape=jax.ShapeDtypeStruct((2, ROWS, M), BF16),
        in_specs=[pl.BlockSpec(memory_space=pltpu.MemorySpace.HBM)] * 2,
        out_specs=VMEM,
        scratch_shapes=[
            pltpu.VMEM((NX, NZ, 3, NY, M), BF16),
            pltpu.VMEM((NX, NY, NZ), F32),
            pltpu.VMEM((4, NX, NZ, 3, NY, M), BF16),
            pltpu.VMEM((NX * NZ * 3, 3 * NY, M), F32),
            pltpu.VMEM((12, 2, CELLS, M), BF16),
            pltpu.VMEM((ROWS, M), BF16),
            pltpu.VMEM((3, ROWS // 4, M), BF16),
            pltpu.VMEM((ROWS // 4, M), BF16),
            pltpu.VMEM((CZ - 1, ROWS // 32, M), BF16),
            pltpu.VMEM((4, ROWS // 32, M), F32),
            pltpu.VMEM((3, 3, M, M), F32),
            pltpu.VMEM((3, TILES, M, M), F32),
            pltpu.VMEM((TILES * M // PACK, PACK, M), BF16),
            pltpu.VMEM((TILES, BLOCK * M // PACK, PACK, M), BF16),
            pltpu.VMEM((TILES, BLOCK * M // PACK, PACK, M), BF16),
            pltpu.SemaphoreType.DMA((2,)),
            pltpu.SemaphoreType.DMA((7 + 4 * FAR,)),
            pltpu.SemaphoreType.DMA((7 + 4 * FAR,)),
            pltpu.SemaphoreType.DMA((len(CHUNKS), COPIES)),
            pltpu.SemaphoreType.DMA((len(CHUNKS), COPIES)),
        ],
        compiler_params=pltpu.CompilerParams(
            collective_id=0, has_side_effects=True, vmem_limit_bytes=40 * 2**20
        ),
        name="tensor",
    )(pltpu.with_memory_space_constraint(phi, pltpu.HBM), pltpu.with_memory_space_constraint(weight, pltpu.HBM))


PARTS = 16


def widen_kernel(src_ref, out_ref, wide, sem):
    count = M * M // PARTS
    copies = []
    for n in range(PARTS):
        wide[n * count : (n + 1) * count, :] = src_ref[n * count : (n + 1) * count, :].astype(F32)
        span = pl.ds(n * count, count)
        copy = pltpu.make_async_copy(wide.at[span], out_ref.at[span], sem.at[n])
        copy.start()
        copies.append(copy)
    for copy in copies:
        copy.wait()


def widen_call(full):
    return pl.pallas_call(
        widen_kernel,
        out_shape=jax.ShapeDtypeStruct((M * M, M), F32),
        in_specs=[VMEM],
        out_specs=pl.BlockSpec(memory_space=pl.ANY),
        scratch_shapes=[pltpu.VMEM((M * M, M), F32), pltpu.SemaphoreType.DMA((PARTS,))],
        compiler_params=pltpu.CompilerParams(vmem_limit_bytes=24 * 2**20),
        name="widen",
    )(full)


def shards(velocity_modes, cell_weight):
    phi = jnp.transpose(velocity_modes, (0, 2, 3, 1, 4))
    full = tensor_call(phi, cell_weight)
    return widen_call(full.reshape(M * M, M)).reshape(M, M, M)


def solution(mesh):
    placed = (P("stream", "span", None, None, None), P("stream", "span", None))
    return jax.shard_map(shards, mesh=mesh, in_specs=placed, out_specs=P(), check_vma=False)
```
